32 devices in a mesh: sep: 4 (over y, x), gx: 8 (over z, core).
Axes of the slice: x: 2, y: 2, z: 4, core: 2. Of those that a mesh axis runs over, the one named last changes fastest.
Arguments:
- velocity: float32 [3, 2048, 8, 128], P(None, 'gx'), may hold values from -6 to 6
- distances: int32 [32], replicated, may hold values from 1 to 2044, as said below
Outputs:
- flux_slope: float32 [32, 2048, 8, 128], P('sep', 'gx')
- transport: float32 [32, 2048, 8, 128], P('sep', 'gx')
The draws below stay inside these ranges and needn't reach their ends.
Inputs may be any that keep to these rules, and one draw needn't show every extreme that they name: `distances`: strictly increasing. In each of the 4 groups of 8 consecutive entries, the last exceeds the first by at most (7) * 4, with equality in some group.
All inputs are finite; a program needn't handle non-finite values.
Results may differ from the reference program's by a relative error of at most 0.0003.
Values sent between devices are 32-bit elements; how exact they have to be, the bound alone decides.
No kernel may reach another device: no remote copies, remote signals or barrier semaphores. Data moves between devices by JAX's collectives and lax.ppermute only.
A program may use at most 128 MiB of HBM per device.

```python
import jax
import jax.numpy as jnp
from jax import lax

NX = 2048
NYW = 8
NZW = 128
SEP_DEV = 8
GAP = 4
SEPS = 32


def draw_distances(key, part):
    groups = SEPS // SEP_DEV
    keys = jax.random.split(jax.random.fold_in(key, 17), 3)
    inner_gaps = jax.random.randint(keys[0], (SEPS,), 1, GAP + 1)
    outer_gaps = jax.random.randint(keys[1], (SEPS,), 1, NX * SEP_DEV // SEPS - (SEP_DEV - 1) * GAP)
    widest = jax.random.randint(keys[2], (), 0, groups)
    position = jnp.arange(SEPS)
    group_of = position // SEP_DEV
    inner_gaps = jnp.where(group_of == widest, GAP, inner_gaps)
    gaps = jnp.where(position % SEP_DEV == 0, outer_gaps, inner_gaps)
    summed = jnp.cumsum(gaps)
    last_first = SEPS - SEP_DEV
    base = NX - groups - (SEP_DEV - 1) * GAP
    final_group = summed - summed[last_first] + base
    result = jnp.where(group_of == groups - 1, final_group, summed)
    return result.astype(jnp.int32)


def block_scale(rng, dims, cuts, least, high):
    loudness, own = 1.0, jax.random.fold_in(rng, 6)
    for dim, parts in cuts:
        steps = jnp.exp(jax.random.uniform(jax.random.fold_in(own, dim), (parts,), jnp.float32, least / len(cuts), high / len(cuts)))
        loudness = loudness * jnp.repeat(steps, dims[dim] // parts).reshape([-1 if axis == dim else 1 for axis in range(len(dims))])
    return loudness


def scatter_about(key, shape, scale, most, cuts=(), held_as=jnp.bfloat16):
    factor_of = block_scale(key, shape, cuts, -0.22, 0.18) if cuts else 1.0
    array = jax.random.normal(key, shape, jnp.float32) * scale * factor_of
    return jnp.minimum(jnp.maximum(array, -most), most).astype(held_as)


def setup_inputs(seed: int = 0) -> dict:
    seeds = jax.random.split(jax.random.key(seed), 3)
    velocity = scatter_about(seeds[0], (3, NX, NYW, NZW), 1.0, 6.0, ((1, 8),), jnp.float32)
    distances = draw_distances(jax.random.fold_in(seeds[2], 71), 0)
    return {"velocity": velocity, "distances": distances}


def shifted(velocity, offset):
    doubled = jnp.concatenate([velocity, velocity], axis=1)
    return lax.dynamic_slice_in_dim(doubled, offset.astype(jnp.int32), NX, 1)


def terms(velocity, offset):
    moved = shifted(velocity, offset)
    change = moved - velocity
    squared = jnp.sum(change * change, axis=0)
    flux = change[0] * squared
    carried = (0.5 * (moved[0] + velocity[0])) * squared
    return flux, carried


def reference(velocity, distances):
    fluxes, carried = lax.map(lambda offset: terms(velocity, offset), distances)
    zero_plane = jnp.zeros_like(fluxes[:1])
    below = jnp.concatenate([zero_plane, fluxes[:-1]], axis=0)
    above = jnp.concatenate([fluxes[1:], fluxes[-1:]], axis=0)
    lower_dist = jnp.concatenate([jnp.zeros((1,), jnp.int32), distances[:-1]], axis=0)
    upper_dist = jnp.concatenate([distances[1:], distances[-1:]], axis=0)
    spread = (upper_dist - lower_dist).astype(jnp.float32)[:, None, None, None]
    flux_slope = (above - below) / spread
    transport = 0.5 * (jnp.roll(carried, -1, axis=1) - jnp.roll(carried, 1, axis=1))
    return flux_slope, transport
```

```python
import jax
import jax.numpy as jnp
from jax import lax
from jax.experimental import pallas as pl
from jax.experimental.pallas import tpu as pltpu
from jax.sharding import PartitionSpec as P

CORES = 2
STEP = 32


def hop(value, axis, pairs):
    return lax.ppermute(value, axis, pairs)


def spread_gather(velocity):
    group = lax.axis_index("sep")
    place = lax.axis_index("gx")
    groups = lax.axis_size("sep")
    count = lax.axis_size("gx")
    chips = count // CORES
    cells = velocity.shape[1]
    part = cells // groups
    half = part // 2
    chip = place // CORES
    core = place % CORES

    def along(value, links):
        pairs = [(a * CORES + c, b * CORES + c) for a, b in links for c in range(CORES)]
        return hop(value, "gx", pairs)

    def across(value, bit):
        return hop(value, "sep", [(s, s ^ bit) for s in range(groups)])

    def partner(value):
        return hop(value, "gx", [(d, d ^ 1) for d in range(count)])

    pair_swap = [(a, a ^ 1) for a in range(chips)]
    mid = [(1, 2), (2, 1)]
    outward = [(1, 0), (2, 3)]
    mine = lax.dynamic_slice_in_dim(velocity, group * part, part, 1)
    first = along(mine, pair_swap)
    inner2 = along(mine, mid)
    outer2 = along(inner2, outward)
    inner3 = along(first, mid)
    outer3 = along(inner3, outward)
    inside = jnp.logical_or(chip == 1, chip == 2)
    second = jnp.where(inside, inner2, outer2)
    third = jnp.where(inside, inner3, outer3)
    low = chip < chips // 2
    near = chip ^ 1
    middle = jnp.where(low, 2, 1)
    far = jnp.where(low, 3, 0)

    pieces = []

    def keep(value, source, offset):
        pieces.append((value, (source * CORES + core) * cells + offset))
        pieces.append((partner(value), (source * CORES + 1 - core) * cells + offset))

    keep(velocity, chip, 0)
    for slot, source in ((first, near), (second, middle), (third, far)):
        by_x = across(slot, 1)
        by_y = across(slot, 2)
        diag_a = across(by_x[:, :half], 2)
        diag_b = across(by_y[:, half:], 1)
        keep(slot, source, group * part)
        keep(by_x, source, (group ^ 1) * part)
        keep(by_y, source, (group ^ 2) * part)
        keep(diag_a, source, (group ^ 3) * part)
        keep(diag_b, source, (group ^ 3) * part + half)
    return pieces


def kernel(scalars, spreads, *refs):
    pieces = refs[:-4]
    slope_ref, transport_ref, field, sems = refs[-4:]
    step = pl.program_id(0)
    total = field.shape[1]
    members = slope_ref.shape[0]
    rows = slope_ref.shape[1]
    fixed = members + 3

    def copies():
        for number, piece in enumerate(pieces):
            planes = piece.shape[1]
            begin = scalars[fixed + number]
            yield pltpu.make_async_copy(
                piece, field.at[:, pl.ds(begin, planes)], sems.at[number]
            )

    @pl.when(step == 0)
    def _():
        for copy in copies():
            copy.start()
        for copy in copies():
            copy.wait()

    origin = scalars[members + 2] + step * rows

    def base_at(x):
        at = (origin + x + total) & (total - 1)
        return at, [field[c, at] for c in range(3)]

    def term(base, at, number):
        there = (at + scalars[number]) & (total - 1)
        moved = [field[c, there] for c in range(3)]
        change = [m - b for m, b in zip(moved, base)]
        squared = change[0] * change[0] + change[1] * change[1] + change[2] * change[2]
        return change[0], squared, moved[0] + base[0]

    def carried_at(x):
        at, base = base_at(x)
        result = []
        for member in range(members):
            _, squared, twice = term(base, at, member + 1)
            result.append(twice * squared)
        return result

    def both_at(x):
        at, base = base_at(x)
        fluxes, carried = [], []
        for member in range(members + 2):
            change, squared, twice = term(base, at, member)
            fluxes.append(change * squared)
            if 0 < member <= members:
                carried.append(twice * squared)
        return fluxes, carried

    def emit(x, fluxes, before, after):
        for member in range(members):
            slope_ref[member, x] = (fluxes[member + 2] - fluxes[member]) * spreads[member]
            transport_ref[member, x] = 0.25 * (after[member] - before[member])

    def body(x, state):
        before, fluxes, now = state[0], state[1], state[2]
        next_fluxes, after = both_at(x + 1)
        emit(x, fluxes, before, after)
        return now, next_fluxes, after

    before = carried_at(-1)
    fluxes, now = both_at(0)
    lax.fori_loop(0, rows, body, (before, fluxes, now), unroll=2)


def body(velocity, distances):
    group = lax.axis_index("sep")
    groups = lax.axis_size("sep")
    place = lax.axis_index("gx")
    cells = velocity.shape[1]
    total = cells * lax.axis_size("gx")
    members = distances.shape[0] // groups
    if groups == 4 and lax.axis_size("gx") == 4 * CORES:
        pieces = spread_gather(velocity)
    else:
        pieces = [(lax.all_gather(velocity, "gx", axis=1, tiled=True), 0)]
    padded = jnp.concatenate([jnp.zeros((1,), jnp.int32), distances, distances[-1:]])
    near = lax.dynamic_slice_in_dim(padded, group * members, members + 2)
    spreads = 1.0 / (near[2:] - near[:-2]).astype(jnp.float32)
    begins = jnp.stack([jnp.asarray(begin, jnp.int32) for _, begin in pieces])
    scalars = jnp.concatenate([near, jnp.stack([place * cells]).astype(jnp.int32), begins])
    shape = (members, cells) + velocity.shape[2:]
    step = min(STEP, cells)
    block = pl.BlockSpec((members, step) + velocity.shape[2:], lambda i: (0, i, 0, 0))
    smem = pl.BlockSpec(memory_space=pltpu.SMEM)
    field = (velocity.shape[0], total) + velocity.shape[2:]
    return pl.pallas_call(
        kernel,
        grid=(cells // step,),
        out_shape=(jax.ShapeDtypeStruct(shape, jnp.float32),) * 2,
        in_specs=[smem, smem] + [pl.BlockSpec(memory_space=pl.ANY)] * len(pieces),
        out_specs=(block, block),
        scratch_shapes=[
            pltpu.VMEM(field, jnp.float32),
            pltpu.SemaphoreType.DMA((len(pieces),)),
        ],
        compiler_params=pltpu.CompilerParams(
            dimension_semantics=("arbitrary",), vmem_limit_bytes=56 << 20
        ),
        name="terms",
    )(scalars, spreads, *[value for value, _ in pieces])


def solution(mesh):
    placed = (P(None, "gx", None, None), P())
    return jax.shard_map(
        body,
        mesh=mesh,
        in_specs=placed,
        out_specs=(P("sep", "gx", None, None), P("sep", "gx", None, None)),
        check_vma=False,
    )
```

```python
import jax
import jax.numpy as jnp
from jax import lax
from jax.experimental import pallas as pl
from jax.experimental.pallas import tpu as pltpu
from jax.sharding import PartitionSpec as P


CORES = 2
ROWS = 32
UNROLL = 4
SLOTS = 4


class Plan:
    def __init__(self, group, groups, place, count, cells):
        self.group, self.groups, self.count = group, groups, count
        self.chips = count // CORES
        self.chip, self.core = place // CORES, place % CORES
        part = cells // groups
        self.chunks = (part * 3 // 8, part // 2)
        self.share = sum(self.chunks)
        self.rest = groups * self.share
        self.cells = cells
        low = self.chip < self.chips // 2
        near = (self.chip ^ 1, jnp.where(low, 2, 1), jnp.where(low, 3, 0))
        self.begins, self.planes = [], []
        self.note(self.chip, 0, cells)
        for source in near:
            self.note(source, self.rest, cells - self.rest)
        for chunk in range(2):
            for source in near:
                for other in (0, 1, 2, 3):
                    begin = (group ^ other) * self.share + chunk * self.chunks[0]
                    self.note(source, begin, self.chunks[chunk])

    def note(self, source, offset, planes):
        for core in (self.core, 1 - self.core):
            self.begins.append((source * CORES + core) * self.cells + offset)
            self.planes.append(planes)

    def gather(self, velocity, distances, make):
        pairs_of = lambda links: [
            (a * CORES + c, b * CORES + c) for a, b in links for c in range(CORES)
        ]

        def along(value, links):
            return lax.ppermute(value, "gx", pairs_of(links))

        def across(value, bit):
            return lax.ppermute(value, "sep", [(s, s ^ bit) for s in range(self.groups)])

        pieces = []

        def keep(value):
            other = lax.ppermute(value, "gx", [(d, d ^ 1) for d in range(self.count)])
            pieces.extend((value, other))

        inside = jnp.logical_or(self.chip == 1, self.chip == 2)
        mid = [(1, 2), (2, 1)]
        outward = [(1, 0), (2, 3)]

        def line(mine):
            first = along(mine, [(a, a ^ 1) for a in range(self.chips)])
            inner2 = along(mine, mid)
            outer2 = along(inner2, outward)
            inner3 = along(first, mid)
            outer3 = along(inner3, outward)
            return first, jnp.where(inside, inner2, outer2), jnp.where(inside, inner3, outer3)

        keep(velocity)
        for value in line(velocity[:, self.rest :]):
            keep(value)
        for chunk in range(2):
            begin = self.group * self.share + chunk * self.chunks[0]
            mine = lax.dynamic_slice_in_dim(velocity, begin, self.chunks[chunk], 1)
            mine, velocity = lax.optimization_barrier((mine, velocity))
            for slot, value in enumerate(line(mine)):
                tag = f"{slot + 1}{chunk + 1}"
                by_x = across(value, 1)
                by_y = across(value, 2)
                if tag == "31":
                    by_y, distances = lax.optimization_barrier((by_y, distances))
                    table = make(distances)
                if tag == "32":
                    by_y, table = lax.optimization_barrier((by_y, table))
                flip = (slot + chunk) % 2
                diagonal = across(by_y, 1) if flip else across(by_x, 2)
                keep(value)
                keep(by_x)
                keep(by_y)
                keep(diagonal)
        return pieces, table


def tuned(groups, count):
    return groups == 4 and count == 4 * CORES


def kernel(table, spreads, *refs):
    pieces = refs[:-6]
    slopes_out, transport_out, field, staged, sems, out_sems = refs[-6:]
    members, cells = slopes_out.shape[:2]
    rows = staged.shape[3]
    spare = rows + 2
    total = field.shape[1] - spare - SPREAD
    count = len(pieces)
    steps = cells // rows
    begins = members + 3
    needs = begins + count
    queue = needs + count
    until = queue + count

    def copies(number):
        piece = pieces[number]
        begin = table[begins + number]
        short = min(piece.shape[1], SPREAD)
        return (
            pltpu.make_async_copy(
                piece, field.at[:, pl.ds(begin, piece.shape[1])], sems.at[0, number]
            ),
            pltpu.make_async_copy(
                piece.at[:, :short], field.at[:, pl.ds(total + begin, short)], sems.at[1, number]
            ),
            begin < spare,
        )

    def start(number, when):
        @pl.when(when)
        def _():
            whole, again, wraps = copies(number)
            whole.start()
            pl.when(wraps)(again.start)

    for number in range(count):
        start(number, table[needs + number] == 0)
    for number in range(count):
        need = table[needs + number]
        start(number, jnp.logical_and(need > 0, need < steps))

    runs = []
    for number, piece in enumerate(pieces):
        if not runs or runs[-1][0] != piece.shape[1]:
            runs.append([piece.shape[1], number, number])
        runs[-1][2] = number

    def wait(position, carry):
        number = table[queue + position]
        wraps = table[begins + number] < spare
        for planes, least, most in runs:

            @pl.when(jnp.logical_and(number >= least, number <= most))
            def _():
                target = field.at[:, pl.ds(0, planes)]
                pltpu.make_async_copy(target, target, sems.at[0, number]).wait()

                @pl.when(wraps)
                def _():
                    target = field.at[:, pl.ds(0, min(planes, SPREAD))]
                    pltpu.make_async_copy(target, target, sems.at[1, number]).wait()

        return carry

    def write(step, slot):
        rows_out = pl.ds(step * rows, rows)
        return [
            pltpu.make_async_copy(
                staged.at[slot, which], out.at[:, rows_out], out_sems.at[slot, which]
            )
            for which, out in enumerate((slopes_out, transport_out))
        ]

    def spots_of(step):
        result = []
        for distance in [0] + [table[number] for number in range(members + 2)]:
            at = table[members + 2] + step * rows + distance + total - 1
            at = jnp.where(at >= total, at - total, at)
            result.append(jnp.where(at >= total, at - total, at))
        return result

    def plane(spots, x, both):
        base = [field[c, spots[0] + (x + 1)] for c in range(3)]
        fluxes, carried = [], []
        for number in range(members + 2):
            inner = 0 < number <= members
            if not (both or inner):
                continue
            moved = [field[c, spots[number + 1] + (x + 1)] for c in range(3)]
            change = [m - b for m, b in zip(moved, base)]
            squared = change[0] * change[0] + change[1] * change[1] + change[2] * change[2]
            if both:
                fluxes.append(change[0] * squared)
            if inner:
                carried.append((moved[0] + base[0]) * squared)
        if not both:
            return carried
        return carried, [
            (fluxes[member + 2] - fluxes[member]) * spreads[member] for member in range(members)
        ]

    def advance(step, state):
        first = jnp.maximum(table[until + step], table[until + 1])
        lax.fori_loop(first, table[until + step + 1], wait, 0)
        slot = step % SLOTS

        @pl.when(step >= SLOTS)
        def _():
            for copy in write(step - SLOTS, slot):
                copy.wait()

        spots = spots_of(step)

        def turn(index, state):
            before, now, slopes = state
            for u in range(UNROLL):
                x = index * UNROLL + u
                after, following = plane(spots, x + 1, True)
                for member in range(members):
                    staged[slot, 0, member, x] = slopes[member]
                    staged[slot, 1, member, x] = 0.25 * (after[member] - before[member])
                before, now, slopes = now, after, following
            return before, now, slopes

        state = lax.fori_loop(0, rows // UNROLL, turn, state)
        for copy in write(step, slot):
            copy.start()
        return state

    lax.fori_loop(table[until], table[until + 1], wait, 0)
    spots = spots_of(0)
    state = (plane(spots, -1, False), *plane(spots, 0, True))
    lax.fori_loop(0, steps, advance, state)
    for step in range(max(0, steps - SLOTS), steps):
        for copy in write(step, step % SLOTS):
            copy.wait()


SPREAD = 64


def table_of(begins, planes, near, origin, total, rows, steps):
    begins = jnp.stack([jnp.asarray(begin, jnp.int32) for begin in begins])
    number = jnp.arange(len(planes))
    begin = begins[:, None, None]
    size = jnp.asarray(planes, jnp.int32)[:, None, None]
    zero = jnp.zeros((), jnp.int32)
    least = jnp.stack([zero, near[0], near[1], near[-1]])
    most = jnp.stack([zero, near[0], near[-2], near[-1]])
    low = origin - 1 + jnp.arange(steps)[None, :, None] * rows + least
    length = (rows + 2 + most - least)[None, None, :]
    hit = jnp.logical_or((begin - low) % total < length, (low - begin) % total < size)
    hit = jnp.any(hit, axis=2)
    needs = jnp.min(jnp.where(hit, jnp.arange(steps)[None, :], steps), axis=1)
    key = needs * len(planes) + number
    rank = jnp.sum(key[None, :] < key[:, None], axis=1)
    queue = jnp.sum(jnp.where(rank[None, :] == number[:, None], number[None, :], 0), axis=1)
    until = jnp.sum(needs[None, :] < jnp.arange(steps + 1)[:, None], axis=1)
    parts = [near, origin[None], begins, needs, queue, until]
    return jnp.concatenate([part.astype(jnp.int32) for part in parts])


def body(velocity, distances):
    group, groups = lax.axis_index("sep"), lax.axis_size("sep")
    place, count = lax.axis_index("gx"), lax.axis_size("gx")
    cells = velocity.shape[1]
    total = cells * count
    members = distances.shape[0] // groups
    rows = min(ROWS, cells)
    steps = cells // rows
    origin = place * cells

    def make(distances):
        padded = jnp.concatenate([jnp.zeros((1,), jnp.int32), distances, distances[-1:]])
        near = lax.dynamic_slice_in_dim(padded, group * members, members + 2)
        spreads = 1.0 / (near[2:] - near[:-2]).astype(jnp.float32)
        return table_of(begins, planes, near, origin, total, rows, steps), spreads

    if tuned(groups, count):
        plan = Plan(group, groups, place, count, cells)
        begins, planes = plan.begins, plan.planes
        pieces, (table, spreads) = plan.gather(velocity, distances, make)
    else:
        begins, planes = [0], [total]
        pieces = [lax.all_gather(velocity, "gx", axis=1, tiled=True)]
        table, spreads = make(distances)
    window = velocity.shape[2:]
    shape = (members, cells) + window
    smem = pl.BlockSpec(memory_space=pltpu.SMEM)
    whole = pl.BlockSpec(memory_space=pl.ANY)
    return pl.pallas_call(
        kernel,
        out_shape=(jax.ShapeDtypeStruct(shape, jnp.float32),) * 2,
        in_specs=[smem, smem] + [whole] * len(pieces),
        out_specs=(whole, whole),
        scratch_shapes=[
            pltpu.VMEM((velocity.shape[0], total + rows + 2 + SPREAD) + window, jnp.float32),
            pltpu.VMEM((SLOTS, 2, members, rows) + window, jnp.float32),
            pltpu.SemaphoreType.DMA((2, len(pieces))),
            pltpu.SemaphoreType.DMA((SLOTS, 2)),
        ],
        compiler_params=pltpu.CompilerParams(vmem_limit_bytes=56 << 20),
        name="terms",
    )(table, spreads, *pieces)


def solution(mesh):
    placed = (P(None, "gx", None, None), P())
    return jax.shard_map(
        body,
        mesh=mesh,
        in_specs=placed,
        out_specs=(P("sep", "gx", None, None), P("sep", "gx", None, None)),
        check_vma=False,
    )
```
